32 devices in a mesh: tok: 4 (over z), feat: 8 (over y, x, core).
Axes of the slice: x: 2, y: 2, z: 4, core: 2. Of those that a mesh axis runs over, the one named last changes fastest.
Arguments:
- activations: bfloat16 [16384, 28672], P('tok', 'feat'), may hold values from -6 to 6
- out_grads: bfloat16 [16384, 8192], P('tok', 'feat'), may hold values from -6 to 6
- query_in: bfloat16 [8, 32, 28672], P('tok', None, 'feat'), may hold values from -0.03125 to 0.03125
- query_out: bfloat16 [8, 32, 8192], P('tok', None, 'feat'), may hold values from -0.0625 to 0.0625
Outputs:
- influence: float32 [8, 16384], P(None, ('tok', 'feat'))
The draws below stay inside these ranges and needn't reach their ends.
All inputs are finite; a program needn't handle non-finite values.
Results may differ from the reference program's by a relative error of at most 0.0003.
Values may be sent and summed in bfloat16 or wider, within the bound.
A program may use at most 128 MiB of HBM per device.

```python
import jax
import jax.numpy as jnp
from jax import lax

FIN = 28672
DOUT = 8192
RANK = 32
TOKENS = 16384
QUERIES = 8


def level_of(own_key, dims, cuts, smallest, top_value):
    factor_of = 1.0
    for position, shards_of in cuts:
        draws = jax.random.uniform(jax.random.fold_in(jax.random.fold_in(own_key, 6), position), (shards_of,), jnp.float32, smallest / len(cuts), top_value / len(cuts))
        factor_of = factor_of * jnp.repeat(jnp.exp(draws), dims[position] // shards_of).reshape((-1,) + (1,) * (len(dims) - 1 - position))
    return factor_of


def scatter_about(stream_key, shape, deviation, limit, cuts=(), held_as=jnp.bfloat16):
    array = jax.random.normal(stream_key, shape, jnp.float32) * deviation
    if len(cuts) > 0:
        array = level_of(stream_key, shape, cuts, -0.22, 0.18) * array
    return jnp.clip(array, min=-limit, max=limit).astype(held_as)


def setup_inputs(seed: int = 0) -> dict:
    key_of = jax.random.split(jax.random.key(seed), 5)
    activations = scatter_about(key_of[0], (TOKENS, FIN), 1.0, 6.0, ((0, 4), (1, 8)))
    out_grads = scatter_about(key_of[1], (TOKENS, DOUT), 1.0, 6.0, ((0, 4), (1, 8)))
    query_in = scatter_about(key_of[2], (QUERIES, RANK, FIN), FIN ** -0.5, 0.03125, ((0, 4), (2, 8)))
    query_out = scatter_about(key_of[3], (QUERIES, RANK, DOUT), DOUT ** -0.5, 0.0625, ((0, 4), (2, 8)))
    return {"activations": activations, "out_grads": out_grads, "query_in": query_in, "query_out": query_out}


def reference(activations, out_grads, query_in, query_out):
    in_flat = query_in.reshape(QUERIES * RANK, FIN)
    out_flat = query_out.reshape(QUERIES * RANK, DOUT)
    in_proj = lax.dot_general(activations, in_flat, (((1,), (1,)), ((), ())), preferred_element_type=jnp.float32)
    out_proj = lax.dot_general(out_grads, out_flat, (((1,), (1,)), ((), ())), preferred_element_type=jnp.float32)
    product = (in_proj * out_proj).reshape(TOKENS, QUERIES, RANK)
    return jnp.sum(product, axis=2).T
```

```python
import functools

import jax
import jax.numpy as jnp
from jax import lax
from jax.experimental import pallas as pl
from jax.experimental.pallas import tpu as pltpu
from jax.sharding import PartitionSpec as P

MESH = pl.DeviceIdType.MESH
NT = (((1,), (1,)), ((), ()))


def kernel(
    n, nf, act, grad, qin, qout, out,
    a_buf, g_buf, fin, fout, acc, from_core, from_chip,
    a_sem, g_sem, own_sem, f_send, f_recv, core_send, core_recv, chip_send, chip_recv,
):
    me = lax.axis_index("tok")
    feat = lax.axis_index("feat")
    nc = nf // 2
    chip = feat // 2
    core = lax.rem(feat, 2)
    partner = chip * 2 + (1 - core)
    rows = acc.shape[2]
    cols = qin.shape[0]
    rank_queries = out.shape[0] // n
    rank = cols // rank_queries

    def peer_chip(shift):
        return lax.rem(chip + shift, nc) * 2

    def load(c, side):
        start = pl.multiple_of((peer_chip(nc - 1 - c) + side) * rows, rows)
        at = pl.ds(start, rows)
        slot = c + jnp.where(side == core, nc, 0)
        return (
            pltpu.make_async_copy(act.at[at], a_buf.at[at], a_sem.at[slot]),
            pltpu.make_async_copy(grad.at[at], g_buf.at[at], g_sem.at[slot]),
        )

    own_in = pltpu.make_async_copy(qin, fin.at[me, pl.ds(0, cols)], own_sem.at[0])
    own_out = pltpu.make_async_copy(qout, fout.at[me, pl.ds(cols, cols)], own_sem.at[1])
    own_in.start()
    own_out.start()
    for side in (1 - core, core):
        for c in range(nc):
            for copy in load(c, side):
                copy.start()

    for b in range(n):
        fin[b, cols:, :] = jnp.zeros((cols, fin.shape[2]), fin.dtype)
        fout[b, :cols, :] = jnp.zeros((cols, fout.shape[2]), fout.dtype)
    out[...] = jnp.zeros_like(out)

    barrier = pltpu.get_barrier_semaphore()
    pl.semaphore_signal(barrier, inc=1, device_id=(me, partner), device_id_type=MESH)
    for shift in range(1, nc):
        pl.semaphore_signal(
            barrier, inc=1, device_id=(me, peer_chip(shift) + core), device_id_type=MESH
        )

    @pl.when(me > 0)
    def _():
        pl.semaphore_signal(barrier, inc=1, device_id=(me - 1, feat), device_id_type=MESH)

    @pl.when(me < n - 1)
    def _():
        pl.semaphore_signal(barrier, inc=1, device_id=(me + 1, feat), device_id_type=MESH)

    beside = jnp.where(me > 0, 1, 0) + jnp.where(me < n - 1, 1, 0)
    pl.semaphore_wait(barrier, nc + beside)

    def pass_on(block, src_in, src_out, to, way):
        return (
            pltpu.make_async_remote_copy(
                src_ref=src_in, dst_ref=fin.at[block, pl.ds(0, cols)],
                send_sem=f_send.at[way, block, 0], recv_sem=f_recv.at[block, 0],
                device_id=(to, feat), device_id_type=MESH,
            ),
            pltpu.make_async_remote_copy(
                src_ref=src_out, dst_ref=fout.at[block, pl.ds(cols, cols)],
                send_sem=f_send.at[way, block, 1], recv_sem=f_recv.at[block, 1],
                device_id=(to, feat), device_id_type=MESH,
            ),
        )

    def forward(block, to, way):
        return pass_on(
            block, fin.at[block, pl.ds(0, cols)], fout.at[block, pl.ds(cols, cols)], to, way
        )

    @pl.when(me < n - 1)
    def _():
        for copy in pass_on(me, qin, qout, me + 1, 0):
            copy.start()

    @pl.when(me > 0)
    def _():
        for copy in pass_on(me, qin, qout, me - 1, 1):
            copy.start()

    inner = jnp.logical_and(me > 0, me < n - 1)

    def await_block(block):
        for copy in forward(block, lax.rem(me + 1, n), 0):
            copy.wait_recv()

    def arrive(d):
        @pl.when(jnp.logical_and(inner, me - d >= 0))
        def _():
            await_block(me - d)
            for copy in forward(me - d, me + 1, 0):
                copy.start()

        @pl.when(jnp.logical_and(inner, me + d <= n - 1))
        def _():
            await_block(me + d)
            for copy in forward(me + d, me - 1, 1):
                copy.start()

    near = jnp.minimum(me, n - 1 - me)
    long_left = me > n - 1 - me

    def block_of(i):
        paired = (i + 1) // 2
        far = i - near
        both = jnp.where(lax.rem(i, 2) == 1, me - paired, me + paired)
        one = jnp.where(long_left, me - far, me + far)
        return jnp.where(i == 0, me, jnp.where(i <= 2 * near, both, one))

    def to_core(i, c):
        return pltpu.make_async_remote_copy(
            src_ref=acc.at[i, c], dst_ref=from_core.at[i, c],
            send_sem=core_send.at[i, c], recv_sem=core_recv.at[i, c],
            device_id=(me, partner), device_id_type=MESH,
        )

    def to_chip(i, c):
        return pltpu.make_async_remote_copy(
            src_ref=acc.at[i, nc + c], dst_ref=from_chip.at[i, c],
            send_sem=chip_send.at[i, c], recv_sem=chip_recv.at[i, c],
            device_id=(me, peer_chip(nc - 1 - c) + core), device_id_type=MESH,
        )

    def project(block, c, side):
        start = pl.multiple_of((peer_chip(nc - 1 - c) + side) * rows, rows)
        at = pl.ds(start, rows)
        return lax.dot_general(
            a_buf[at, :], fin[block], NT, preferred_element_type=jnp.float32
        ) + lax.dot_general(
            g_buf[at, :], fout[block], NT, preferred_element_type=jnp.float32
        )

    def finish(i):
        block = block_of(i)
        total = acc[i, 2 * nc - 1]
        for c in range(nc - 1):
            to_chip(i, c).wait_recv()
            total = total + from_chip[i, c]
        product = total * pltpu.roll(total, cols, 1)
        lane = lax.broadcasted_iota(jnp.int32, (out.shape[0], 2 * cols), 1)
        row = lax.broadcasted_iota(jnp.int32, (out.shape[0], 2 * cols), 0)
        first = (row - block * rank_queries) * rank
        mine = (lane >= first) & (lane < first + rank) & (lane < cols)
        chosen = jnp.where(mine, 1.0, 0.0).astype(jnp.float32)
        out[...] += lax.dot_general(
            chosen, product, NT, preferred_element_type=jnp.float32,
            precision=lax.Precision.HIGHEST,
        )

    def slot(i, carry):
        block = block_of(i)

        @pl.when(i == 0)
        def _():
            own_in.wait()
            own_out.wait()

        @pl.when(jnp.logical_and(i > 0, jnp.logical_not(inner)))
        def _():
            await_block(block)

        @pl.when(i == 1)
        def _():
            arrive(1)

        def theirs(c, carry):
            @pl.when(i == 0)
            def _():
                for copy in load(c, 1 - core):
                    copy.wait()

            acc[i, c] = project(block, c, 1 - core)
            to_core(i, c).start()
            return carry

        lax.fori_loop(0, nc, theirs, 0)

        @pl.when(i > 0)
        def _():
            finish(i - 1)

        @pl.when(jnp.logical_and(i >= 2, i <= n - 2))
        def _():
            arrive(i)

        def ours(c, carry):
            @pl.when(i == 0)
            def _():
                for copy in load(c, core):
                    copy.wait()

            mine = project(block, c, core)
            to_core(i, c).wait_recv()
            acc[i, nc + c] = mine + from_core[i, c]

            @pl.when(c < nc - 1)
            def _():
                to_chip(i, c).start()

            return carry

        lax.fori_loop(0, nc, ours, 0)
        return carry

    lax.fori_loop(0, n, slot, 0)
    finish(n - 1)

    def drain(i, carry):
        def cores(c, carry):
            to_core(i, c).wait_send()
            return carry

        def chips(c, carry):
            to_chip(i, c).wait_send()
            return carry

        lax.fori_loop(0, nc, cores, 0)
        lax.fori_loop(0, nc - 1, chips, 0)
        return carry

    lax.fori_loop(0, n, drain, 0)

    def drain_blocks(b, carry):
        @pl.when(jnp.logical_and(me < n - 1, b <= me))
        def _():
            for copy in forward(b, lax.rem(me + 1, n), 0):
                copy.wait_send()

        @pl.when(jnp.logical_and(me > 0, b >= me))
        def _():
            for copy in forward(b, lax.rem(me + 1, n), 1):
                copy.wait_send()

        return carry

    lax.fori_loop(0, n, drain_blocks, 0)


def local(n, nf, activations, out_grads, query_in, query_out):
    per_device, rank, in_local = query_in.shape
    out_local = query_out.shape[2]
    cols = per_device * rank
    tokens = activations.shape[0]
    rows = tokens // nf
    nc = nf // 2
    dma = pltpu.SemaphoreType.DMA
    any_space = pl.BlockSpec(memory_space=pl.ANY)
    return pl.pallas_call(
        functools.partial(kernel, n, nf),
        out_shape=jax.ShapeDtypeStruct((n * per_device, rows), jnp.float32),
        in_specs=[any_space] * 4,
        out_specs=pl.BlockSpec(memory_space=pltpu.VMEM),
        scratch_shapes=[
            pltpu.VMEM((tokens, in_local), activations.dtype),
            pltpu.VMEM((tokens, out_local), out_grads.dtype),
            pltpu.VMEM((n, 2 * cols, in_local), query_in.dtype),
            pltpu.VMEM((n, 2 * cols, out_local), query_out.dtype),
            pltpu.VMEM((n, nf, rows, 2 * cols), jnp.float32),
            pltpu.VMEM((n, nc, rows, 2 * cols), jnp.float32),
            pltpu.VMEM((n, nc - 1, rows, 2 * cols), jnp.float32),
            dma((nf,)),
            dma((nf,)),
            dma((2,)),
            dma((2, n, 2)),
            dma((n, 2)),
            dma((n, nc)),
            dma((n, nc)),
            dma((n, nc - 1)),
            dma((n, nc - 1)),
        ],
        compiler_params=pltpu.CompilerParams(
            collective_id=0, has_side_effects=True, vmem_limit_bytes=66_000_000
        ),
    )(
        activations, out_grads,
        query_in.reshape(cols, in_local), query_out.reshape(cols, out_local),
    )


def solution(mesh):
    n, nf = mesh.shape["tok"], mesh.shape["feat"]
    in_specs = (P("tok", "feat"), P("tok", "feat"), P("tok", None, "feat"), P("tok", None, "feat"))
    out_specs = P(None, ("tok", "feat"))
    return jax.shard_map(
        functools.partial(local, n, nf),
        mesh=mesh, in_specs=in_specs, out_specs=out_specs, check_vma=False,
    )
```

```python
import functools

import jax
import jax.numpy as jnp
from jax import lax
from jax.experimental import pallas as pl
from jax.experimental.pallas import tpu as pltpu
from jax.sharding import PartitionSpec as P

MESH = pl.DeviceIdType.MESH
RELAY = 1
NT = (((1,), (1,)), ((), ()))


def kernel(
    n, nf, act, grad, qin, qout, out,
    a_buf, g_buf, fin, fout, acc, from_core, x_first, y_first, y_last, x_last,
    a_sem, g_sem, own_sem, f_send, f_recv, core_send, core_recv,
    xf_send, xf_recv, yf_send, yf_recv, yl_send, yl_recv, xl_send, xl_recv,
):
    me = lax.axis_index("tok")
    feat = lax.axis_index("feat")
    nc = nf // 2
    chip = feat // 2
    core = lax.rem(feat, 2)
    partner = chip * 2 + (1 - core)
    rows = acc.shape[2]
    cols = qin.shape[0]
    rank_queries = out.shape[0] // n
    rank = cols // rank_queries

    ny = nc // 2
    half = rows // 2
    x, y = lax.rem(chip, 2), chip // 2

    def peer(dy, dx):
        return (lax.rem(y + dy, ny) * 2 + lax.rem(x + dx, 2)) * 2

    def peer_at(c):
        return peer(lax.rem(ny - 1 - lax.rem(c, ny) + ny, ny), jnp.where(c < ny, 1, 0))

    def load(c, side):
        start = pl.multiple_of((peer_at(c) + side) * rows, rows)
        at = pl.ds(start, rows)
        slot = c + jnp.where(side == core, nc, 0)
        return (
            pltpu.make_async_copy(act.at[at], a_buf.at[at], a_sem.at[slot]),
            pltpu.make_async_copy(grad.at[at], g_buf.at[at], g_sem.at[slot]),
        )

    own_in = pltpu.make_async_copy(qin, fin.at[me, pl.ds(0, cols)], own_sem.at[0])
    own_out = pltpu.make_async_copy(qout, fout.at[me, pl.ds(cols, cols)], own_sem.at[1])
    own_in.start()
    own_out.start()
    for side in (1 - core, core):
        for c in range(nc):
            for copy in load(c, side):
                copy.start()

    for b in range(n):
        fin[b, cols:, :] = jnp.zeros((cols, fin.shape[2]), fin.dtype)
        fout[b, :cols, :] = jnp.zeros((cols, fout.shape[2]), fout.dtype)
    out[...] = jnp.zeros_like(out)

    barrier = pltpu.get_barrier_semaphore()
    pl.semaphore_signal(barrier, inc=1, device_id=(me, partner), device_id_type=MESH)
    for dy in range(1, ny):
        pl.semaphore_signal(
            barrier, inc=1, device_id=(me, peer(dy, 0) + core), device_id_type=MESH
        )
    pl.semaphore_signal(barrier, inc=1, device_id=(me, peer(0, 1) + core), device_id_type=MESH)

    @pl.when(me > 0)
    def _():
        pl.semaphore_signal(barrier, inc=1, device_id=(me - 1, feat), device_id_type=MESH)

    @pl.when(me < n - 1)
    def _():
        pl.semaphore_signal(barrier, inc=1, device_id=(me + 1, feat), device_id_type=MESH)

    beside = jnp.where(me > 0, 1, 0) + jnp.where(me < n - 1, 1, 0)
    pl.semaphore_wait(barrier, ny + 1 + beside)

    def pass_on(block, src_in, src_out, to, way):
        return (
            pltpu.make_async_remote_copy(
                src_ref=src_in, dst_ref=fin.at[block, pl.ds(0, cols)],
                send_sem=f_send.at[way, block, 0], recv_sem=f_recv.at[block, 0],
                device_id=(to, feat), device_id_type=MESH,
            ),
            pltpu.make_async_remote_copy(
                src_ref=src_out, dst_ref=fout.at[block, pl.ds(cols, cols)],
                send_sem=f_send.at[way, block, 1], recv_sem=f_recv.at[block, 1],
                device_id=(to, feat), device_id_type=MESH,
            ),
        )

    def forward(block, to, way):
        return pass_on(
            block, fin.at[block, pl.ds(0, cols)], fout.at[block, pl.ds(cols, cols)], to, way
        )

    @pl.when(me < n - 1)
    def _():
        for copy in pass_on(me, qin, qout, me + 1, 0):
            copy.start()

    @pl.when(me > 0)
    def _():
        for copy in pass_on(me, qin, qout, me - 1, 1):
            copy.start()

    inner = jnp.logical_and(me > 0, me < n - 1)

    def await_block(block):
        for copy in forward(block, lax.rem(me + 1, n), 0):
            copy.wait_recv()

    def arrive(d):
        @pl.when(jnp.logical_and(inner, me - d >= 0))
        def _():
            await_block(me - d)
            for copy in forward(me - d, me + 1, 0):
                copy.start()

        @pl.when(jnp.logical_and(inner, me + d <= n - 1))
        def _():
            await_block(me + d)
            for copy in forward(me + d, me - 1, 1):
                copy.start()

    near = jnp.minimum(me, n - 1 - me)
    long_left = me > n - 1 - me

    def block_of(i):
        paired = (i + 1) // 2
        far = i - near
        both = jnp.where(lax.rem(i, 2) == 1, me - paired, me + paired)
        one = jnp.where(long_left, me - far, me + far)
        return jnp.where(i == 0, me, jnp.where(i <= 2 * near, both, one))

    def to_core(i, c):
        return pltpu.make_async_remote_copy(
            src_ref=acc.at[i, c], dst_ref=from_core.at[i, c],
            send_sem=core_send.at[i, c], recv_sem=core_recv.at[i, c],
            device_id=(me, partner), device_id_type=MESH,
        )

    top, low = pl.ds(0, half), pl.ds(half, half)

    def send(src, dst, send_sem, recv_sem, dy, dx):
        return pltpu.make_async_remote_copy(
            src_ref=src, dst_ref=dst, send_sem=send_sem, recv_sem=recv_sem,
            device_id=(me, peer(dy, dx) + core), device_id_type=MESH,
        )

    def along_x(i, dy):
        return send(
            acc.at[i, nc + ny - 1 - dy, top], x_first.at[i, dy],
            xf_send.at[i, dy], xf_recv.at[i, dy], 0, 1,
        )

    def along_y(i, dy, dx):
        return send(
            acc.at[i, 2 * nc - 1 - dx * ny - dy, low], y_first.at[i, dy - 1, dx],
            yf_send.at[i, dy - 1, dx], yf_recv.at[i, dy - 1, dx], dy, 0,
        )

    def then_y(i, dy):
        return send(
            acc.at[i, 2 * nc - 1 - dy, top], y_last.at[i, dy - 1],
            yl_send.at[i, dy - 1], yl_recv.at[i, dy - 1], dy, 0,
        )

    def then_x(i):
        return send(
            acc.at[i, nc + ny - 1, low], x_last.at[i], xl_send.at[i], xl_recv.at[i], 0, 1
        )

    def relay(i):
        for dy in range(ny - 1, 0, -1):
            along_x(i, dy).wait_recv()
            acc[i, 2 * nc - 1 - dy, :half, :] += x_first[i, dy]
            then_y(i, dy).start()
        total = acc[i, nc + ny - 1, half:, :]
        for dy in range(ny - 1, 0, -1):
            along_y(i, dy, 1).wait_recv()
            total = total + y_first[i, dy - 1, 1]
        acc[i, nc + ny - 1, half:, :] = total
        then_x(i).start()

    def project(block, c, side):
        start = pl.multiple_of((peer_at(c) + side) * rows, rows)
        at = pl.ds(start, rows)
        return lax.dot_general(
            a_buf[at, :], fin[block], NT, preferred_element_type=jnp.float32
        ) + lax.dot_general(
            g_buf[at, :], fout[block], NT, preferred_element_type=jnp.float32
        )

    def finish(i):
        block = block_of(i)
        along_x(i, 0).wait_recv()
        upper = acc[i, 2 * nc - 1, :half, :] + x_first[i, 0]
        lower = acc[i, 2 * nc - 1, half:, :]
        for dy in range(ny - 1, 0, -1):
            along_y(i, dy, 0).wait_recv()
            lower = lower + y_first[i, dy - 1, 0]
        for dy in range(ny - 1, 0, -1):
            then_y(i, dy).wait_recv()
            upper = upper + y_last[i, dy - 1]
        then_x(i).wait_recv()
        lower = lower + x_last[i]
        total = jnp.concatenate([upper, lower], axis=0)
        product = total * pltpu.roll(total, cols, 1)
        lane = lax.broadcasted_iota(jnp.int32, (out.shape[0], 2 * cols), 1)
        row = lax.broadcasted_iota(jnp.int32, (out.shape[0], 2 * cols), 0)
        first = (row - block * rank_queries) * rank
        mine = (lane >= first) & (lane < first + rank) & (lane < cols)
        chosen = jnp.where(mine, 1.0, 0.0).astype(jnp.float32)
        out[...] += lax.dot_general(
            chosen, product, NT, preferred_element_type=jnp.float32,
            precision=lax.Precision.HIGHEST,
        )

    def slot(i, carry):
        block = block_of(i)

        @pl.when(i == 0)
        def _():
            own_in.wait()
            own_out.wait()

        @pl.when(jnp.logical_and(i > 0, jnp.logical_not(inner)))
        def _():
            await_block(block)

        @pl.when(i == 1)
        def _():
            arrive(1)

        def theirs(c, carry):
            @pl.when(i == 0)
            def _():
                for copy in load(c, 1 - core):
                    copy.wait()

            acc[i, c] = project(block, c, 1 - core)
            to_core(i, c).start()
            return carry

        lax.fori_loop(0, nc, theirs, 0)

        @pl.when(i > 1)
        def _():
            finish(i - 2)

        @pl.when(jnp.logical_and(i >= 2, i <= n - 2))
        def _():
            arrive(i)

        def ours(c, carry):
            @pl.when(i == 0)
            def _():
                for copy in load(c, core):
                    copy.wait()

            mine = project(block, c, core)
            to_core(i, c).wait_recv()
            acc[i, nc + c] = mine + from_core[i, c]

            for k in range(nc - 1):
                dx, dy = 1 - k // ny, ny - 1 - k % ny

                @pl.when(c == k)
                def _():
                    if dx:
                        along_x(i, dy).start()
                    if dy:
                        along_y(i, dy, dx).start()

            @pl.when(jnp.logical_and(i > 0, c == RELAY))
            def _():
                relay(i - 1)

            return carry

        lax.fori_loop(0, nc, ours, 0)
        return carry

    lax.fori_loop(0, n, slot, 0)
    finish(n - 2)
    relay(n - 1)
    finish(n - 1)

    def drain(i, carry):
        def cores(c, carry):
            to_core(i, c).wait_send()
            return carry

        for dy in range(ny):
            along_x(i, dy).wait_send()
        for dy in range(1, ny):
            along_y(i, dy, 0).wait_send()
            along_y(i, dy, 1).wait_send()
            then_y(i, dy).wait_send()
        then_x(i).wait_send()

        lax.fori_loop(0, nc, cores, 0)
        return carry

    lax.fori_loop(0, n, drain, 0)

    def drain_blocks(b, carry):
        @pl.when(jnp.logical_and(me < n - 1, b <= me))
        def _():
            for copy in forward(b, lax.rem(me + 1, n), 0):
                copy.wait_send()

        @pl.when(jnp.logical_and(me > 0, b >= me))
        def _():
            for copy in forward(b, lax.rem(me + 1, n), 1):
                copy.wait_send()

        return carry

    lax.fori_loop(0, n, drain_blocks, 0)


def local(n, nf, activations, out_grads, query_in, query_out):
    per_device, rank, in_local = query_in.shape
    out_local = query_out.shape[2]
    cols = per_device * rank
    tokens = activations.shape[0]
    rows = tokens // nf
    nc = nf // 2
    ny = nc // 2
    dma = pltpu.SemaphoreType.DMA
    any_space = pl.BlockSpec(memory_space=pl.ANY)
    return pl.pallas_call(
        functools.partial(kernel, n, nf),
        out_shape=jax.ShapeDtypeStruct((n * per_device, rows), jnp.float32),
        in_specs=[any_space] * 4,
        out_specs=pl.BlockSpec(memory_space=pltpu.VMEM),
        scratch_shapes=[
            pltpu.VMEM((tokens, in_local), activations.dtype),
            pltpu.VMEM((tokens, out_local), out_grads.dtype),
            pltpu.VMEM((n, 2 * cols, in_local), query_in.dtype),
            pltpu.VMEM((n, 2 * cols, out_local), query_out.dtype),
            pltpu.VMEM((n, nf, rows, 2 * cols), jnp.float32),
            pltpu.VMEM((n, nc, rows, 2 * cols), jnp.float32),
            pltpu.VMEM((n, ny, rows // 2, 2 * cols), jnp.float32),
            pltpu.VMEM((n, ny - 1, 2, rows // 2, 2 * cols), jnp.float32),
            pltpu.VMEM((n, ny - 1, rows // 2, 2 * cols), jnp.float32),
            pltpu.VMEM((n, rows // 2, 2 * cols), jnp.float32),
            dma((nf,)),
            dma((nf,)),
            dma((2,)),
            dma((2, n, 2)),
            dma((n, 2)),
            dma((n, nc)),
            dma((n, nc)),
            dma((n, ny)),
            dma((n, ny)),
            dma((n, ny - 1, 2)),
            dma((n, ny - 1, 2)),
            dma((n, ny - 1)),
            dma((n, ny - 1)),
            dma((n,)),
            dma((n,)),
        ],
        compiler_params=pltpu.CompilerParams(
            collective_id=0, has_side_effects=True, vmem_limit_bytes=66_000_000
        ),
    )(
        activations, out_grads,
        query_in.reshape(cols, in_local), query_out.reshape(cols, out_local),
    )


def solution(mesh):
    n, nf = mesh.shape["tok"], mesh.shape["feat"]
    in_specs = (P("tok", "feat"), P("tok", "feat"), P("tok", None, "feat"), P("tok", None, "feat"))
    out_specs = P(None, ("tok", "feat"))
    return jax.shard_map(
        functools.partial(local, n, nf),
        mesh=mesh, in_specs=in_specs, out_specs=out_specs, check_vma=False,
    )
```

```python
import functools

import jax
import jax.numpy as jnp
from jax import lax
from jax.experimental import pallas as pl
from jax.experimental.pallas import tpu as pltpu
from jax.sharding import PartitionSpec as P

MESH = pl.DeviceIdType.MESH
RELAY = 1
PASS_ON = 2
NT = (((1,), (1,)), ((), ()))


def kernel(
    n, nf, act, grad, qin, qout, out,
    a_buf, g_buf, fin, fout, acc, from_core, x_first, y_first, y_last, x_last,
    a_sem, g_sem, own_sem, f_send, f_recv, core_send, core_recv,
    xf_send, xf_recv, yf_send, yf_recv, yl_send, yl_recv, xl_send, xl_recv,
):
    me = lax.axis_index("tok")
    feat = lax.axis_index("feat")
    nc = nf // 2
    chip = feat // 2
    core = lax.rem(feat, 2)
    partner = chip * 2 + (1 - core)
    rows = acc.shape[2]
    cols = qin.shape[0]
    rank_queries = out.shape[0] // n
    rank = cols // rank_queries

    ny = nc // 2
    half = rows // 2
    x, y = lax.rem(chip, 2), chip // 2

    def peer(dy, dx):
        return (lax.rem(y + dy, ny) * 2 + lax.rem(x + dx, 2)) * 2

    def peer_at(c):
        return peer(lax.rem(ny - 1 - lax.rem(c, ny) + ny, ny), jnp.where(c < ny, 1, 0))

    def load(c, side):
        start = pl.multiple_of((peer_at(c) + side) * rows, rows)
        at = pl.ds(start, rows)
        slot = c + jnp.where(side == core, nc, 0)
        return (
            pltpu.make_async_copy(act.at[at], a_buf.at[at], a_sem.at[slot]),
            pltpu.make_async_copy(grad.at[at], g_buf.at[at], g_sem.at[slot]),
        )

    own_in = pltpu.make_async_copy(qin, fin.at[me], own_sem.at[0])
    own_out = pltpu.make_async_copy(qout, fout.at[me], own_sem.at[1])
    own_in.start()
    own_out.start()
    for side in (1 - core, core):
        for c in range(nc):
            for copy in load(c, side):
                copy.start()

    out[...] = jnp.zeros_like(out)

    barrier = pltpu.get_barrier_semaphore()
    pl.semaphore_signal(barrier, inc=1, device_id=(me, partner), device_id_type=MESH)
    for dy in range(1, ny):
        pl.semaphore_signal(
            barrier, inc=1, device_id=(me, peer(dy, 0) + core), device_id_type=MESH
        )
    pl.semaphore_signal(barrier, inc=1, device_id=(me, peer(0, 1) + core), device_id_type=MESH)

    @pl.when(me > 0)
    def _():
        pl.semaphore_signal(barrier, inc=1, device_id=(me - 1, feat), device_id_type=MESH)

    @pl.when(me < n - 1)
    def _():
        pl.semaphore_signal(barrier, inc=1, device_id=(me + 1, feat), device_id_type=MESH)

    beside = jnp.where(me > 0, 1, 0) + jnp.where(me < n - 1, 1, 0)
    pl.semaphore_wait(barrier, ny + 1 + beside)

    def pass_on(block, src_in, src_out, to, way):
        return (
            pltpu.make_async_remote_copy(
                src_ref=src_in, dst_ref=fin.at[block],
                send_sem=f_send.at[way, block, 0], recv_sem=f_recv.at[block, 0],
                device_id=(to, feat), device_id_type=MESH,
            ),
            pltpu.make_async_remote_copy(
                src_ref=src_out, dst_ref=fout.at[block],
                send_sem=f_send.at[way, block, 1], recv_sem=f_recv.at[block, 1],
                device_id=(to, feat), device_id_type=MESH,
            ),
        )

    def forward(block, to, way):
        return pass_on(
            block, fin.at[block], fout.at[block], to, way
        )

    @pl.when(me < n - 1)
    def _():
        for copy in pass_on(me, qin, qout, me + 1, 0):
            copy.start()

    @pl.when(me > 0)
    def _():
        for copy in pass_on(me, qin, qout, me - 1, 1):
            copy.start()

    inner = jnp.logical_and(me > 0, me < n - 1)

    def await_block(block):
        for copy in forward(block, lax.rem(me + 1, n), 0):
            copy.wait_recv()

    def arrive(d):
        @pl.when(jnp.logical_and(inner, me - d >= 0))
        def _():
            await_block(me - d)
            for copy in forward(me - d, me + 1, 0):
                copy.start()

        @pl.when(jnp.logical_and(inner, me + d <= n - 1))
        def _():
            await_block(me + d)
            for copy in forward(me + d, me - 1, 1):
                copy.start()

    near = jnp.minimum(me, n - 1 - me)
    long_left = me > n - 1 - me

    def block_of(i):
        paired = (i + 1) // 2
        far = i - near
        both = jnp.where(lax.rem(i, 2) == 1, me - paired, me + paired)
        one = jnp.where(long_left, me - far, me + far)
        return jnp.where(i == 0, me, jnp.where(i <= 2 * near, both, one))

    def to_core(i, c):
        return pltpu.make_async_remote_copy(
            src_ref=acc.at[i, c], dst_ref=from_core.at[i, c],
            send_sem=core_send.at[i, c], recv_sem=core_recv.at[i, c],
            device_id=(me, partner), device_id_type=MESH,
        )

    top, low = pl.ds(0, half), pl.ds(half, half)

    def send(src, dst, send_sem, recv_sem, dy, dx):
        return pltpu.make_async_remote_copy(
            src_ref=src, dst_ref=dst, send_sem=send_sem, recv_sem=recv_sem,
            device_id=(me, peer(dy, dx) + core), device_id_type=MESH,
        )

    def along_x(i, dy):
        return send(
            acc.at[i, nc + ny - 1 - dy, top], x_first.at[i, dy],
            xf_send.at[i, dy], xf_recv.at[i, dy], 0, 1,
        )

    def along_y(i, dy, dx):
        return send(
            acc.at[i, 2 * nc - 1 - dx * ny - dy, low], y_first.at[i, dy - 1, dx],
            yf_send.at[i, dy - 1, dx], yf_recv.at[i, dy - 1, dx], dy, 0,
        )

    def then_y(i, dy):
        return send(
            acc.at[i, 2 * nc - 1 - dy, top], y_last.at[i, dy - 1],
            yl_send.at[i, dy - 1], yl_recv.at[i, dy - 1], dy, 0,
        )

    def then_x(i):
        return send(
            acc.at[i, nc + ny - 1, low], x_last.at[i], xl_send.at[i], xl_recv.at[i], 0, 1
        )

    def relay(i):
        for dy in range(ny - 1, 0, -1):
            along_x(i, dy).wait_recv()
            acc[i, 2 * nc - 1 - dy, :half, :] += x_first[i, dy]
            then_y(i, dy).start()
        total = acc[i, nc + ny - 1, half:, :]
        for dy in range(ny - 1, 0, -1):
            along_y(i, dy, 1).wait_recv()
            total = total + y_first[i, dy - 1, 1]
        acc[i, nc + ny - 1, half:, :] = total
        then_x(i).start()

    def project(block, c, side):
        start = pl.multiple_of((peer_at(c) + side) * rows, rows)
        at = pl.ds(start, rows)
        in_side = lax.dot_general(
            a_buf[at, :], fin[block], NT, preferred_element_type=jnp.float32
        )
        out_side = lax.dot_general(
            g_buf[at, :], fout[block], NT, preferred_element_type=jnp.float32
        )
        return jnp.concatenate([in_side, out_side], axis=1)

    def finish(i):
        block = block_of(i)
        along_x(i, 0).wait_recv()
        upper = acc[i, 2 * nc - 1, :half, :] + x_first[i, 0]
        lower = acc[i, 2 * nc - 1, half:, :]
        for dy in range(ny - 1, 0, -1):
            along_y(i, dy, 0).wait_recv()
            lower = lower + y_first[i, dy - 1, 0]
        for dy in range(ny - 1, 0, -1):
            then_y(i, dy).wait_recv()
            upper = upper + y_last[i, dy - 1]
        then_x(i).wait_recv()
        lower = lower + x_last[i]
        total = jnp.concatenate([upper, lower], axis=0)
        product = total * pltpu.roll(total, cols, 1)
        lane = lax.broadcasted_iota(jnp.int32, (out.shape[0], 2 * cols), 1)
        row = lax.broadcasted_iota(jnp.int32, (out.shape[0], 2 * cols), 0)
        first = (row - block * rank_queries) * rank
        mine = (lane >= first) & (lane < first + rank) & (lane < cols)
        chosen = jnp.where(mine, 1.0, 0.0).astype(jnp.float32)
        out[...] += lax.dot_general(
            chosen, product, NT, preferred_element_type=jnp.float32,
            precision=lax.Precision.HIGHEST,
        )

    def slot(i, carry):
        block = block_of(i)

        @pl.when(i == 0)
        def _():
            own_in.wait()
            own_out.wait()

        @pl.when(jnp.logical_and(i > 0, jnp.logical_not(inner)))
        def _():
            await_block(block)

        def theirs(c, carry):
            @pl.when(i == 0)
            def _():
                for copy in load(c, 1 - core):
                    copy.wait()

            acc[i, c] = project(block, c, 1 - core)
            to_core(i, c).start()
            return carry

        lax.fori_loop(0, nc, theirs, 0)

        @pl.when(i > 1)
        def _():
            finish(i - 2)

        def ours(c, carry):
            @pl.when(i == 0)
            def _():
                for copy in load(c, core):
                    copy.wait()

            @pl.when(jnp.logical_and(i < n - 2, c == PASS_ON))
            def _():
                arrive(i + 1)

            mine = project(block, c, core)
            to_core(i, c).wait_recv()
            acc[i, nc + c] = mine + from_core[i, c]

            for k in range(nc - 1):
                dx, dy = 1 - k // ny, ny - 1 - k % ny

                @pl.when(c == k)
                def _():
                    if dx:
                        along_x(i, dy).start()
                    if dy:
                        along_y(i, dy, dx).start()

            @pl.when(jnp.logical_and(i > 0, c == RELAY))
            def _():
                relay(i - 1)

            return carry

        lax.fori_loop(0, nc, ours, 0)
        return carry

    lax.fori_loop(0, n, slot, 0)
    relay(n - 1)
    finish(n - 2)
    finish(n - 1)

    def drain(i, carry):
        def cores(c, carry):
            to_core(i, c).wait_send()
            return carry

        for dy in range(ny):
            along_x(i, dy).wait_send()
        for dy in range(1, ny):
            along_y(i, dy, 0).wait_send()
            along_y(i, dy, 1).wait_send()
            then_y(i, dy).wait_send()
        then_x(i).wait_send()

        lax.fori_loop(0, nc, cores, 0)
        return carry

    lax.fori_loop(0, n, drain, 0)

    def drain_blocks(b, carry):
        @pl.when(jnp.logical_and(me < n - 1, b <= me))
        def _():
            for copy in forward(b, lax.rem(me + 1, n), 0):
                copy.wait_send()

        @pl.when(jnp.logical_and(me > 0, b >= me))
        def _():
            for copy in forward(b, lax.rem(me + 1, n), 1):
                copy.wait_send()

        return carry

    lax.fori_loop(0, n, drain_blocks, 0)


def local(n, nf, activations, out_grads, query_in, query_out):
    per_device, rank, in_local = query_in.shape
    out_local = query_out.shape[2]
    cols = per_device * rank
    tokens = activations.shape[0]
    rows = tokens // nf
    nc = nf // 2
    ny = nc // 2
    dma = pltpu.SemaphoreType.DMA
    any_space = pl.BlockSpec(memory_space=pl.ANY)
    return pl.pallas_call(
        functools.partial(kernel, n, nf),
        out_shape=jax.ShapeDtypeStruct((n * per_device, rows), jnp.float32),
        in_specs=[any_space] * 4,
        out_specs=pl.BlockSpec(memory_space=pltpu.VMEM),
        scratch_shapes=[
            pltpu.VMEM((tokens, in_local), activations.dtype),
            pltpu.VMEM((tokens, out_local), out_grads.dtype),
            pltpu.VMEM((n, cols, in_local), query_in.dtype),
            pltpu.VMEM((n, cols, out_local), query_out.dtype),
            pltpu.VMEM((n, nf, rows, 2 * cols), jnp.float32),
            pltpu.VMEM((n, nc, rows, 2 * cols), jnp.float32),
            pltpu.VMEM((n, ny, rows // 2, 2 * cols), jnp.float32),
            pltpu.VMEM((n, ny - 1, 2, rows // 2, 2 * cols), jnp.float32),
            pltpu.VMEM((n, ny - 1, rows // 2, 2 * cols), jnp.float32),
            pltpu.VMEM((n, rows // 2, 2 * cols), jnp.float32),
            dma((nf,)),
            dma((nf,)),
            dma((2,)),
            dma((2, n, 2)),
            dma((n, 2)),
            dma((n, nc)),
            dma((n, nc)),
            dma((n, ny)),
            dma((n, ny)),
            dma((n, ny - 1, 2)),
            dma((n, ny - 1, 2)),
            dma((n, ny - 1)),
            dma((n, ny - 1)),
            dma((n,)),
            dma((n,)),
        ],
        compiler_params=pltpu.CompilerParams(
            collective_id=0, has_side_effects=True, vmem_limit_bytes=66_000_000
        ),
    )(
        activations, out_grads,
        query_in.reshape(cols, in_local), query_out.reshape(cols, out_local),
    )


def solution(mesh):
    n, nf = mesh.shape["tok"], mesh.shape["feat"]
    in_specs = (P("tok", "feat"), P("tok", "feat"), P("tok", None, "feat"), P("tok", None, "feat"))
    out_specs = P(None, ("tok", "feat"))
    return jax.shard_map(
        functools.partial(local, n, nf),
        mesh=mesh, in_specs=in_specs, out_specs=out_specs, check_vma=False,
    )
```
